32 devices in a mesh: grp: 8 (over z, x), blk: 4 (over y, core).
Axes of the slice: x: 2, y: 2, z: 4, core: 2. Of those that a mesh axis runs over, the one named last changes fastest.
Arguments:
- raw_ints: bfloat16 [2048, 32, 512], P('grp', 'blk'), may hold values from -0.59765625 to 0.59765625
- metric: bfloat16 [2048, 2048], P(None, 'grp'), as said below
- occ_energy: float32 [32], replicated, may hold values from -2 to -0.3
- virt_energy: float32 [512], replicated, may hold values from 0.2 to 5
Outputs:
- density: float32 [2048, 32, 512], P(None, ('blk', 'grp'))
- pair_energy: float32 [32, 4], P(('blk', 'grp'))
The draws below stay inside these ranges and needn't reach their ends.
Inputs may be any that keep to these rules, and one draw needn't show every extreme that they name: `metric`: Symmetric.
All inputs are finite; a program needn't handle non-finite values.
Results may differ from the reference program's by a relative error of at most 0.0033.
Values may be sent and summed in bfloat16 or wider, within the bound.
No kernel may reach another device: no remote copies, remote signals or barrier semaphores. Data moves between devices by JAX's collectives and lax.ppermute only.
A program may use at most 128 MiB of HBM per device.

```python
import math
import jax
import jax.numpy as jnp
from jax import lax

NAUX = 2048
NV = 512
VISITS = 4
NOCC = 32
N_GRP = 8
N_BLK = 4


def draw_metric(key, part):
    first, second = jax.random.split(jax.random.fold_in(key, 7))
    noise = jax.random.normal(first, (NAUX, NAUX), jnp.float32)
    noise = (noise + noise.T) * (0.6 / jnp.sqrt(2.0 * NAUX))
    diag = 1.0 + 0.3 * jax.random.uniform(second, (NAUX,), jnp.float32)
    return (noise + jnp.diag(diag)).astype(jnp.bfloat16)


def block_scale(own_key, shape, cuts, low, largest):
    def one(axis_at, parts):
        steps = jax.random.uniform(jax.random.fold_in(jax.random.fold_in(own_key, 6), axis_at), (parts,), jnp.float32, low / len(cuts), largest / len(cuts))
        return jnp.repeat(jnp.exp(steps), shape[axis_at] // parts).reshape((-1,) + (1,) * (len(shape) - axis_at - 1))

    loudness = one(*cuts[0])
    for cut in cuts[1:]:
        loudness = loudness * one(*cut)
    return loudness


def bell_draw(stream_key, extent, scale, bound, shards=(), kind=jnp.bfloat16):
    drawn = scale * jax.random.normal(stream_key, extent, jnp.float32)
    if shards:
        drawn = drawn * block_scale(stream_key, extent, shards, -0.22, 0.18)
    return jnp.clip(drawn, -bound, bound).astype(kind)


def setup_inputs(seed: int = 0) -> dict:
    streams_of = jax.random.split(jax.random.key(seed), 5)
    return {
        "raw_ints": bell_draw(streams_of[0], (NAUX, NOCC, NV), 0.08, 0.59765625, ((0, 8), (1, 4))),
        "metric": draw_metric(jax.random.fold_in(streams_of[4], 71), 0),
        "occ_energy": jnp.clip(jax.random.uniform(streams_of[2], (NOCC,), jnp.float32, -2.0, -0.3), -2.0, -0.3),
        "virt_energy": jnp.clip(jnp.exp(jax.random.uniform(streams_of[3], (NV,), jnp.float32, math.log(0.2), math.log(5.0))), 0.2, 5.0),
    }


def chain_orbital(place):
    return (place % N_BLK) * N_GRP + place // N_BLK


def reference(raw_ints, metric, occ_energy, virt_energy):
    metric_wide = metric.astype(jnp.float32)

    def fit_one(orbital):
        block = lax.dynamic_index_in_dim(raw_ints, orbital, 1, keepdims=False).astype(jnp.float32)
        return jnp.dot(metric_wide, block, precision=lax.Precision.HIGHEST).astype(jnp.bfloat16)

    fitted = lax.map(fit_one, jnp.arange(NOCC, dtype=jnp.int32))

    def per_orbital(orbital):
        place = (orbital % N_GRP) * N_BLK + orbital // N_GRP
        own = lax.dynamic_index_in_dim(fitted, orbital, 0, keepdims=False).astype(jnp.float32)
        e_own = occ_energy[orbital]
        total = jnp.zeros((NAUX, NV), jnp.float32)
        energies = []
        for step in range(VISITS):
            if step == 0:
                partner = place
            else:
                partner = jnp.where((place - step) % 2 == 0, (place - step) % NOCC, (place + step) % NOCC)
            other_orb = chain_orbital(partner).astype(jnp.int32)
            other = lax.dynamic_index_in_dim(fitted, other_orb, 0, keepdims=False).astype(jnp.float32)
            coulomb = jnp.einsum("qa,qb->ab", own, other, precision=lax.Precision.HIGHEST)
            denom = e_own + occ_energy[other_orb] - virt_energy[:, None] - virt_energy[None, :]
            amplitude = coulomb / denom
            tilde = 2.0 * amplitude - amplitude.T
            energies.append(jnp.sum(coulomb * tilde))
            tilde_low = tilde.astype(jnp.bfloat16).astype(jnp.float32)
            total = total + jnp.einsum("qb,ab->qa", other, tilde_low, precision=lax.Precision.HIGHEST)
        return total, jnp.stack(energies)

    density, pair_energy = lax.map(per_orbital, jnp.arange(NOCC, dtype=jnp.int32))
    return jnp.transpose(density, (1, 0, 2)), pair_energy
```

```python
import functools

import jax
import jax.numpy as jnp
from jax import lax
from jax.experimental import pallas as pl
from jax.experimental.pallas import tpu as pltpu
from jax.sharding import PartitionSpec as P

VISITS = 4
BF16, F32 = jnp.bfloat16, jnp.float32
BOTH = ("grp", "blk")
VMEM_CAP = 56 * 2**20


def params():
    return pltpu.CompilerParams(vmem_limit_bytes=VMEM_CAP)


def swapped(value, axis, mask):
    pairs = [(source, source ^ mask) for source in range(lax.axis_size(axis))]
    return lax.ppermute(value, axis, pairs)


def forwarded(value):
    total = lax.axis_size(BOTH)
    pairs = [(p, (p + 2) % total if p % 2 == 0 else (p - 2) % total) for p in range(total)]
    return lax.ppermute(value, BOTH, pairs)


def pack_kernel(index_ref, block_ref, out_ref):
    out_ref[...] = block_ref[...]


def pack(metric, index, n_grp):
    rows, cols = metric.shape
    chunk = rows // n_grp // 4
    count = n_grp // 2 + 1
    return pl.pallas_call(
        pack_kernel,
        grid_spec=pltpu.PrefetchScalarGridSpec(
            num_scalar_prefetch=1,
            grid=(count,),
            in_specs=[pl.BlockSpec((chunk, cols), lambda j, i: (((i[0] + j) % n_grp) * 4 + i[1], 0))],
            out_specs=pl.BlockSpec((chunk, cols), lambda j, i: (j, 0)),
        ),
        out_shape=jax.ShapeDtypeStruct((count * chunk, cols), metric.dtype),
        name="pack",
    )(index, metric)


def unpack_kernel(n_grp, index_ref, *refs):
    parts, out_ref = refs[:-1], refs[-1]
    width = out_ref.shape[0] // n_grp
    chunk = width // 4
    g, q = index_ref[0], index_ref[1]

    def place(m, carry):
        for at, part in enumerate(parts):
            odd, dq = at % 2, at // 2
            s = g ^ (2 * m + odd)
            cols = pl.ds(pl.multiple_of(s * width, width), width)
            for j in range(n_grp // 2 + 1):
                a = (s + j) % n_grp
                rows = pl.ds(pl.multiple_of(a * width + (q ^ dq) * chunk, chunk), chunk)
                out_ref[rows, cols] = part[m, j * chunk : (j + 1) * chunk, :]
        return carry

    lax.fori_loop(0, n_grp // 2, place, 0)

    def mirror(s, carry):
        here = pl.ds(pl.multiple_of(s * width, width), width)
        for j in range(1, n_grp // 2):
            there = pl.ds(pl.multiple_of(((s + j) % n_grp) * width, width), width)
            out_ref[here, there] = out_ref[there, here].T
        return carry

    lax.fori_loop(0, n_grp, mirror, 0)


def unpack(parts, index, n_grp):
    width = parts[0].shape[2]
    size = n_grp * width
    whole = pl.BlockSpec(memory_space=pltpu.VMEM)
    return pl.pallas_call(
        functools.partial(unpack_kernel, n_grp),
        in_specs=[pl.BlockSpec(memory_space=pltpu.SMEM)] + [whole] * len(parts),
        out_specs=whole,
        out_shape=jax.ShapeDtypeStruct((size, size), parts[0].dtype),
        compiler_params=params(),
        cost_estimate=pl.CostEstimate(flops=0, bytes_accessed=4 * size * size, transcendentals=0),
        name="unpack",
    )(index, *parts)


def fit_kernel(per, cols_ref, metric_ref, *refs):
    groups, out_ref, acc_ref = refs[:-2], refs[-2], refs[-1]
    step = pl.program_id(0)
    for at, group in enumerate(groups):

        @pl.when(step // per == at)
        def _():
            part = jnp.dot(metric_ref[...], group[0], preferred_element_type=F32)

            @pl.when(step == 0)
            def _():
                acc_ref[...] = part

            @pl.when(step > 0)
            def _():
                acc_ref[...] += part

    @pl.when(step == pl.num_programs(0) - 1)
    def _():
        out_ref[...] = acc_ref[...].astype(BF16)


def fit(metric, groups, cols):
    size = metric.shape[0]
    per, width, nv = groups[0].shape
    count = len(groups) * per

    def block_of(at):
        return lambda i, c: (jnp.clip(i - at * per, 0, per - 1), 0, 0)

    return pl.pallas_call(
        functools.partial(fit_kernel, per),
        grid_spec=pltpu.PrefetchScalarGridSpec(
            num_scalar_prefetch=1,
            grid=(count,),
            in_specs=[pl.BlockSpec((size, width), lambda i, c: (0, c[i]))]
            + [pl.BlockSpec((1, width, nv), block_of(at)) for at in range(len(groups))],
            out_specs=pl.BlockSpec((size, nv), lambda i, c: (0, 0)),
            scratch_shapes=[pltpu.VMEM((size, nv), F32)],
        ),
        out_shape=jax.ShapeDtypeStruct((size, nv), BF16),
        compiler_params=params(),
        cost_estimate=pl.CostEstimate(
            flops=2 * size * size * nv, bytes_accessed=2 * size * size + 4 * size * nv, transcendentals=0
        ),
        name="fit",
    )(cols, metric, *groups)


def tilde_into(tilde_ref, amp_ref, coulomb_ref, esum, virt_row, virt_col):
    nv = amp_ref.shape[0]
    slab = 128
    for r in range(0, nv, slab):
        denom = esum - virt_col[r : r + slab, :] - virt_row[...]
        amp_ref[r : r + slab, :] = coulomb_ref[r : r + slab, :] / denom
    energy = jnp.float32(0)
    for r in range(0, nv, slab):
        tilde = 2.0 * amp_ref[r : r + slab, :] - amp_ref[:, r : r + slab].T
        energy += jnp.sum(coulomb_ref[r : r + slab, :] * tilde)
        tilde_ref[r : r + slab, :] = tilde.astype(BF16)
    return energy


def pair_kernel(n_new, n_old, has_base, dense, final, tiles, *refs):
    refs = list(refs)
    esum_ref, virt_row, virt_col, own_ref = refs[:4]
    refs = refs[4:]
    new = [refs.pop(0) for _ in range(n_new)]
    old = [refs.pop(0) for _ in range(n_old)]
    old_tilde = [refs.pop(0) for _ in range(n_old)]
    base_ref = refs.pop(0) if has_base else None
    energy_ref = refs.pop(0)
    if dense:
        dens_ref = refs.pop(0)
        tildes = None
    else:
        tildes = [refs.pop(0) for _ in range(n_new)]
    coulombs = [refs.pop(0) for _ in range(n_new)]
    amp_ref = refs.pop(0)
    if dense:
        tildes = [refs.pop(0) for _ in range(n_new)]
    step = pl.program_id(0)

    @pl.when(step < tiles)
    def _():
        for other, coulomb in zip(new, coulombs):
            part = lax.dot_general(
                own_ref[...], other[...], (((0,), (0,)), ((), ())), preferred_element_type=F32
            )

            @pl.when(step == 0)
            def _():
                coulomb[...] = part

            @pl.when(step > 0)
            def _():
                coulomb[...] += part

    @pl.when(step == tiles - 1)
    def _():
        for at in range(n_new):
            energy_ref[0, at] = tilde_into(
                tildes[at], amp_ref, coulombs[at], esum_ref[0, at], virt_row, virt_col
            )

    if dense:

        @pl.when(step >= tiles)
        def _():
            total = base_ref[...] if has_base else None
            for other, tilde in list(zip(old, old_tilde)) + list(zip(new, tildes)):
                part = lax.dot_general(
                    other[...], tilde[...], (((1,), (1,)), ((), ())), preferred_element_type=F32
                )
                total = part if total is None else total + part
            if final:
                lanes = dens_ref.shape[1]
                ways = total.shape[1] // lanes
                for c in range(ways):
                    dens_ref[pl.ds(c, total.shape[0], stride=ways), :] = total[:, c * lanes : (c + 1) * lanes]
            else:
                dens_ref[...] = total


def pairs(own, new, esums, virt, old=(), old_tilde=(), base=None, dense=True, final=False):
    size, nv = own.shape
    tiles = 4
    rows = size // tiles
    n_new, n_old = len(new), len(old)
    first = pl.BlockSpec((rows, nv), lambda i: (jnp.minimum(i, tiles - 1), 0))
    second = pl.BlockSpec((rows, nv), lambda i: (jnp.maximum(i - tiles, 0), 0))
    twice = pl.BlockSpec((rows, nv), lambda i: (i % tiles, 0))
    square = pl.BlockSpec((nv, nv), lambda i: (0, 0))
    in_specs = [
        pl.BlockSpec(memory_space=pltpu.SMEM),
        pl.BlockSpec((1, nv), lambda i: (0, 0)),
        pl.BlockSpec((nv, 1), lambda i: (0, 0)),
        first,
    ]
    in_specs += [twice if dense else first] * n_new + [second] * n_old + [square] * n_old
    args = [esums, virt[None, :], virt[:, None], own, *new, *old, *old_tilde]
    if base is not None:
        in_specs.append(second)
        args.append(base)
    out_specs = [pl.BlockSpec(memory_space=pltpu.SMEM)]
    out_shape = [jax.ShapeDtypeStruct((1, n_new), F32)]
    scratch = [pltpu.VMEM((nv, nv), F32)] * (n_new + 1)
    if dense:
        if final:
            ways = nv // 128
            out_specs.append(pl.BlockSpec((rows * ways, 128), lambda i: (jnp.maximum(i - tiles, 0), 0)))
            out_shape.append(jax.ShapeDtypeStruct((size * ways, 128), F32))
        else:
            out_specs.append(second)
            out_shape.append(jax.ShapeDtypeStruct((size, nv), F32))
        scratch += [pltpu.VMEM((nv, nv), BF16)] * n_new
    else:
        out_specs += [square] * n_new
        out_shape += [jax.ShapeDtypeStruct((nv, nv), BF16)] * n_new
    work = n_new + (n_new + n_old if dense else 0)
    return pl.pallas_call(
        functools.partial(pair_kernel, n_new, n_old, base is not None, dense, final, tiles),
        grid=(2 * tiles if dense else tiles,),
        in_specs=in_specs,
        out_specs=out_specs,
        out_shape=out_shape,
        scratch_shapes=scratch,
        compiler_params=params(),
        cost_estimate=pl.CostEstimate(
            flops=2 * size * nv * nv * work, bytes_accessed=8 * size * nv, transcendentals=0
        ),
        name="pairs",
    )(*args)


def local(raw_ints, metric, occ_energy, virt_energy):
    n_grp = lax.axis_size("grp")
    n_blk = lax.axis_size("blk")
    total = n_grp * n_blk
    g, b = lax.axis_index("grp"), lax.axis_index("blk")
    place = g * n_blk + b
    index = jnp.stack([g, b % 4]).astype(jnp.int32)

    by_orbital = lax.optimization_barrier(jnp.transpose(raw_ints, (1, 0, 2)))
    blocks = [lax.dynamic_index_in_dim(by_orbital, g ^ k, 0, keepdims=False) for k in range(n_grp)]
    half = n_grp // 2
    order = list(range(half, n_grp)) + list(range(1, half))
    got = {0: blocks[0]}
    for k in order:
        got[k] = swapped(blocks[k], "grp", k)
    near = jnp.stack([got[k] for k in range(half)])
    far = jnp.stack([got[k] for k in range(half, n_grp)])
    near_next, far_next = forwarded(near), forwarded(far)

    mine = pack(metric, index, n_grp)
    even = jnp.stack([mine] + [swapped(mine, "grp", k) for k in range(2, n_grp, 2)])
    odd = swapped(even, "grp", 1)
    even_y = swapped(even, "blk", 2)
    odd_y = swapped(odd, "blk", 2)
    parts = [even, odd]
    parts += [swapped(even, "blk", 1), swapped(odd, "blk", 1), even_y, odd_y]
    parts += [swapped(even_y, "blk", 1), swapped(odd_y, "blk", 1)]
    full = unpack(parts, index, n_grp)

    steps = jnp.arange(n_grp, dtype=jnp.int32)
    own = fit(full, [near, far], (g ^ steps).astype(jnp.int32))
    mate = swapped(own, "blk", 1)
    source = jnp.where(place % 2 == 0, (place - 2) % total, (place + 2) % total) // n_blk
    next_ = fit(full, [near_next, far_next], (source ^ steps).astype(jnp.int32))
    next_mate = swapped(next_, "blk", 1)

    spot = jnp.arange(VISITS, dtype=jnp.int32)
    down, up = (place - spot) % total, (place + spot) % total
    partner = jnp.where((place - spot) % 2 == 0, down, up)
    orbital = partner % n_blk * n_grp + partner // n_blk
    energies = occ_energy[orbital]
    esum = (energies[0] + energies)[None, :]

    energy_a, base = pairs(own, [own, mate], esum[:, :2], virt_energy)
    energy_b, tilde_b = pairs(own, [next_], esum[:, 2:3], virt_energy, dense=False)
    energy_c, density = pairs(
        own, [next_mate], esum[:, 3:4], virt_energy, old=[next_], old_tilde=[tilde_b], base=base, final=True
    )
    size, nv = own.shape
    energy = jnp.concatenate([energy_a, energy_b, energy_c], axis=1)
    return density.reshape(size, 1, nv), energy


def solution(mesh):
    in_specs = (P("grp", "blk", None), P(None, "grp"), P(), P())
    out_specs = (P(None, ("blk", "grp"), None), P(("blk", "grp"), None))
    return jax.shard_map(local, mesh=mesh, in_specs=in_specs, out_specs=out_specs, check_vma=False)
```

```python
import functools

import jax
import jax.numpy as jnp
from jax import lax
from jax.experimental import pallas as pl
from jax.experimental.pallas import tpu as pltpu
from jax.sharding import PartitionSpec as P

VISITS = 4
GROUPS = 4
BF16, F32 = jnp.bfloat16, jnp.float32
BOTH = ("grp", "blk")
VMEM_CAP = 56 * 2**20
SMEM = pl.BlockSpec(memory_space=pltpu.SMEM)
VMEM = pl.BlockSpec(memory_space=pltpu.VMEM)
ANY = pl.BlockSpec(memory_space=pl.ANY)
GRP, QUARTER, SOURCE, ORBITAL = 0, 1, 2, 3


def params():
    return pltpu.CompilerParams(vmem_limit_bytes=VMEM_CAP)


def cost(flops, moved):
    return pl.CostEstimate(flops=flops, bytes_accessed=moved, transcendentals=0)


def swapped(value, axis, mask):
    pairs = [(source, source ^ mask) for source in range(lax.axis_size(axis))]
    return lax.ppermute(value, axis, pairs)


def forwarded(value):
    total = lax.axis_size(BOTH)
    pairs = [(p, (p + 2) % total if p % 2 == 0 else (p - 2) % total) for p in range(total)]
    return lax.ppermute(value, BOTH, pairs)


def table_of_integers():
    n_grp, n_blk = lax.axis_size("grp"), lax.axis_size("blk")
    total = n_grp * n_blk
    g, b = lax.axis_index("grp"), lax.axis_index("blk")
    place = g * n_blk + b
    source = jnp.where(place % 2 == 0, (place - 2) % total, (place + 2) % total) // n_blk
    slot = jnp.arange(8, dtype=jnp.int32)
    spot = slot - ORBITAL
    partner = jnp.where((place - spot) % 2 == 0, (place - spot) % total, (place + spot) % total)
    orbital = partner % n_blk * n_grp + partner // n_blk
    table = jnp.where(slot == GRP, g, jnp.where(slot == QUARTER, b % 4, jnp.where(slot == SOURCE, source, orbital)))
    return table.astype(jnp.int32)


def pack_kernel(n_grp, table_ref, metric_ref, out_ref, sems):
    chunk = metric_ref.shape[0] // n_grp // 4
    copies = []
    for j in range(n_grp // 2 + 1):
        row = (((table_ref[GRP] + j) % n_grp) * 4 + table_ref[QUARTER]) * chunk
        copies.append(
            pltpu.make_async_copy(
                metric_ref.at[pl.ds(pl.multiple_of(row, chunk), chunk), :],
                out_ref.at[pl.ds(j * chunk, chunk), :],
                sems.at[j],
            )
        )
        copies[-1].start()
    for copy in copies:
        copy.wait()


def pack(metric, table, n_grp):
    rows, cols = metric.shape
    count = n_grp // 2 + 1
    return pl.pallas_call(
        functools.partial(pack_kernel, n_grp),
        in_specs=[SMEM, ANY],
        out_specs=VMEM,
        out_shape=jax.ShapeDtypeStruct((count * (rows // n_grp // 4), cols), metric.dtype),
        scratch_shapes=[pltpu.SemaphoreType.DMA((count,))],
        name="pack",
    )(table, metric)


def unpack_kernel(n_grp, table_ref, *refs):
    parts, out_ref = refs[:-1], refs[-1]
    width = out_ref.shape[0] // n_grp
    chunk = width // 4
    g, q = table_ref[GRP], table_ref[QUARTER]

    def place(m, carry):
        for at, part in enumerate(parts):
            odd, dq = at % 2, at // 2
            s = g ^ (2 * m + odd)
            cols = pl.ds(pl.multiple_of(s * width, width), width)
            for j in range(n_grp // 2 + 1):
                a = (s + j) % n_grp
                rows = pl.ds(pl.multiple_of(a * width + (q ^ dq) * chunk, chunk), chunk)
                out_ref[rows, cols] = part[m, j * chunk : (j + 1) * chunk, :]
        return carry

    lax.fori_loop(0, n_grp // 2, place, 0)

    def mirror(s, carry):
        here = pl.ds(pl.multiple_of(s * width, width), width)
        for j in range(1, n_grp // 2):
            there = pl.ds(pl.multiple_of(((s + j) % n_grp) * width, width), width)
            out_ref[here, there] = out_ref[there, here].T
        return carry

    lax.fori_loop(0, n_grp, mirror, 0)


def unpack(parts, table, n_grp):
    width = parts[0].shape[2]
    size = n_grp * width
    return pl.pallas_call(
        functools.partial(unpack_kernel, n_grp),
        in_specs=[SMEM] + [VMEM] * len(parts),
        out_specs=VMEM,
        out_shape=jax.ShapeDtypeStruct((size, size), parts[0].dtype),
        compiler_params=params(),
        cost_estimate=cost(0, 4 * size * size),
        name="unpack",
    )(table, *parts)


def fit_kernel(which, has_base, partial, table_ref, metric_ref, *refs):
    refs = list(refs)
    base_ref = refs.pop(0) if has_base else None
    acc_ref = refs.pop()
    out_ref = refs.pop()
    groups = refs
    step = pl.program_id(0)
    per = groups[0].shape[0]
    low = table_ref[which] % per
    for at, group in enumerate(groups):

        @pl.when(step == at)
        def _():
            raw = jnp.concatenate([group[j ^ low] for j in range(per)], axis=0)
            part = jnp.dot(metric_ref[...], raw, preferred_element_type=F32)
            if at == 0 and has_base:
                part = part + base_ref[...]
            if at > 0:
                part = part + acc_ref[...]
            if at < len(groups) - 1:
                acc_ref[...] = part
            else:
                out_ref[...] = part.astype(out_ref.dtype)


def fit(metric, groups, table, which, first=0, base=None, partial=False):
    size = metric.shape[0]
    per, width, nv = groups[0].shape
    fixed = pl.BlockSpec((per, width, nv), lambda i, t: (0, 0, 0))
    whole = pl.BlockSpec((size, nv), lambda i, t: (0, 0))
    return pl.pallas_call(
        functools.partial(fit_kernel, which, base is not None, partial),
        grid_spec=pltpu.PrefetchScalarGridSpec(
            num_scalar_prefetch=1,
            grid=(len(groups),),
            in_specs=[pl.BlockSpec((size, per * width), lambda i, t: (0, (t[which] // per) ^ (i + first)))]
            + ([whole] if base is not None else [])
            + [fixed] * len(groups),
            out_specs=whole,
            scratch_shapes=[pltpu.VMEM((size, nv), F32)],
        ),
        out_shape=jax.ShapeDtypeStruct((size, nv), F32 if partial else BF16),
        compiler_params=params(),
        cost_estimate=cost(2 * size * per * width * nv * len(groups), 2 * size * per * width * len(groups)),
        name="fit",
    )(table, metric, *(() if base is None else (base,)), *groups)


def tilde_into(tilde_ref, amp_ref, coulomb_ref, esum, virt_ref):
    nv = amp_ref.shape[0]
    slab = 128
    cuts = range(0, nv, slab)
    for r in cuts:
        mine = jnp.broadcast_to(virt_ref[:, r : r + slab], (slab, slab)).T
        for c in cuts:
            denom = esum - mine - virt_ref[:, c : c + slab]
            amp_ref[r : r + slab, c : c + slab] = coulomb_ref[r : r + slab, c : c + slab] / denom
    energy = jnp.float32(0)
    for r in cuts:
        tilde = 2.0 * amp_ref[r : r + slab, :] - amp_ref[:, r : r + slab].T
        energy += jnp.sum(coulomb_ref[r : r + slab, :] * tilde)
        tilde_ref[r : r + slab, :] = tilde.astype(BF16)
    return energy


def pair_kernel(visits, n_old, has_base, dense, final, known, tiles, *refs):
    refs = list(refs)
    take = lambda count: [refs.pop(0) for _ in range(count)]
    table_ref, occ_ref, virt_ref, own_ref = take(4)
    new = take(len(visits))
    old, old_tilde = take(n_old), take(n_old)
    base_ref = take(1)[0] if has_base else None
    known_refs = take(len(known))
    energy_ref = take(1)[0]
    dens_ref = take(1)[0] if dense else None
    tildes = take(len(visits)) if not dense else None
    coulombs = take(len(visits))
    amp_ref = take(1)[0]
    if dense:
        tildes = take(len(visits))
    step = pl.program_id(0)

    @pl.when(step < tiles)
    def _():
        for other, coulomb in zip(new, coulombs):
            part = lax.dot_general(
                own_ref[...], other[...], (((0,), (0,)), ((), ())), preferred_element_type=F32
            )

            @pl.when(step == 0)
            def _():
                coulomb[...] = part

            @pl.when(step > 0)
            def _():
                coulomb[...] += part

    @pl.when(step == tiles - 1)
    def _():
        e_own = occ_ref[table_ref[ORBITAL]]
        for ref, (start, count) in zip(known_refs, known):
            for i in range(count):
                energy_ref[0, start + i] = ref[0, i]
        for at, visit in enumerate(visits):
            esum = e_own + occ_ref[table_ref[ORBITAL + visit]]
            energy = tilde_into(tildes[at], amp_ref, coulombs[at], esum, virt_ref)
            energy_ref[0, visit if final else at] = energy

    if dense:

        @pl.when(step >= tiles)
        def _():
            total = base_ref[...] if has_base else None
            for other, tilde in list(zip(old, old_tilde)) + list(zip(new, tildes)):
                part = lax.dot_general(
                    other[...], tilde[...], (((1,), (1,)), ((), ())), preferred_element_type=F32
                )
                total = part if total is None else total + part
            if final:
                lanes = dens_ref.shape[1]
                ways = total.shape[1] // lanes
                for c in range(ways):
                    dens_ref[pl.ds(c, total.shape[0], stride=ways), :] = total[:, c * lanes : (c + 1) * lanes]
            else:
                dens_ref[...] = total


def pairs(own, new, visits, table, occ, virt, old=(), old_tilde=(), base=None, dense=True, final=False, known=()):
    size, nv = own.shape
    tiles = 2
    rows = size // tiles
    n_new, n_old = len(new), len(old)
    first = pl.BlockSpec((rows, nv), lambda i: (jnp.minimum(i, tiles - 1), 0))
    second = pl.BlockSpec((rows, nv), lambda i: (jnp.maximum(i - tiles, 0), 0))
    twice = pl.BlockSpec((rows, nv), lambda i: (i % tiles, 0))
    square = pl.BlockSpec((nv, nv), lambda i: (0, 0))
    in_specs = [SMEM, SMEM, pl.BlockSpec((1, nv), lambda i: (0, 0)), first]
    in_specs += [twice if dense else first] * n_new + [second] * n_old + [square] * n_old
    args = [table, occ, virt, own, *new, *old, *old_tilde]
    if base is not None:
        in_specs.append(second)
        args.append(base)
    in_specs += [SMEM] * len(known)
    args += [energy for _, _, energy in known]
    out_specs = [SMEM]
    out_shape = [jax.ShapeDtypeStruct((1, VISITS if final else n_new), F32)]
    scratch = [pltpu.VMEM((nv, nv), F32)] * (n_new + 1)
    if dense:
        if final:
            ways = nv // 128
            out_specs.append(pl.BlockSpec((rows * ways, 128), lambda i: (jnp.maximum(i - tiles, 0), 0)))
            out_shape.append(jax.ShapeDtypeStruct((size * ways, 128), F32))
        else:
            out_specs.append(second)
            out_shape.append(jax.ShapeDtypeStruct((size, nv), F32))
        scratch += [pltpu.VMEM((nv, nv), BF16)] * n_new
    else:
        out_specs += [square] * n_new
        out_shape += [jax.ShapeDtypeStruct((nv, nv), BF16)] * n_new
    work = n_new + (n_new + n_old if dense else 0)
    return pl.pallas_call(
        functools.partial(
            pair_kernel,
            tuple(visits),
            n_old,
            base is not None,
            dense,
            final,
            tuple((start, count) for start, count, _ in known),
            tiles,
        ),
        grid=(2 * tiles if dense else tiles,),
        in_specs=in_specs,
        out_specs=out_specs,
        out_shape=out_shape,
        scratch_shapes=scratch,
        compiler_params=params(),
        cost_estimate=cost(2 * size * nv * nv * work, 8 * size * nv),
        name="pairs",
    )(*args)


def body(raw_ints, metric, occ_energy, virt_energy):
    n_grp = lax.axis_size("grp")
    per = n_grp // GROUPS
    g = lax.axis_index("grp")
    table = table_of_integers()

    mine = pack(metric, table, n_grp)
    even = jnp.stack([mine] + [swapped(mine, "grp", k) for k in range(2, n_grp, 2)])
    odd = swapped(even, "grp", 1)
    even_y = swapped(even, "blk", 2)
    odd_y = swapped(odd, "blk", 2)
    parts = [even, odd, swapped(even, "blk", 1), swapped(odd, "blk", 1), even_y, odd_y]
    parts += [swapped(even_y, "blk", 1), swapped(odd_y, "blk", 1)]
    full = unpack(parts, table, n_grp)

    by_orbital = lax.optimization_barrier(jnp.transpose(raw_ints, (1, 0, 2)))
    got = [lax.dynamic_index_in_dim(by_orbital, g ^ k, 0, keepdims=False) for k in range(n_grp)]
    got = got[:1] + [swapped(got[k], "grp", k) for k in range(1, n_grp)]
    groups = [jnp.stack(got[i * per : (i + 1) * per]) for i in range(GROUPS)]
    next_groups = [forwarded(group) for group in groups]

    own = fit(full, groups, table, GRP)
    mate = swapped(own, "blk", 1)
    some = fit(full, next_groups[:-1], table, SOURCE, partial=True)
    next_ = fit(full, next_groups[-1:], table, SOURCE, first=GROUPS - 1, base=some)
    next_mate = swapped(next_, "blk", 1)

    virt = virt_energy[None, :]
    energy_a, base = pairs(own, [own, mate], [0, 1], table, occ_energy, virt)
    energy_b, tilde_b = pairs(own, [next_], [2], table, occ_energy, virt, dense=False)
    energy, density = pairs(
        own,
        [next_mate],
        [3],
        table,
        occ_energy,
        virt,
        old=[next_],
        old_tilde=[tilde_b],
        base=base,
        final=True,
        known=[(0, 2, energy_a), (2, 1, energy_b)],
    )
    size, nv = own.shape
    return density.reshape(size, 1, nv), energy


def solution(mesh):
    in_specs = (P("grp", "blk", None), P(None, "grp"), P(), P())
    out_specs = (P(None, ("blk", "grp"), None), P(("blk", "grp"), None))
    return jax.shard_map(body, mesh=mesh, in_specs=in_specs, out_specs=out_specs, check_vma=False)
```

```python
import functools

import jax
import jax.numpy as jnp
from jax import lax
from jax.experimental import pallas as pl
from jax.experimental.pallas import tpu as pltpu
from jax.sharding import PartitionSpec as P

VISITS = 4
GROUPS = 4
BF16, F32 = jnp.bfloat16, jnp.float32
BOTH = ("grp", "blk")
VMEM_CAP = 16 * 2**20
TILE = 512
SMEM = pl.BlockSpec(memory_space=pltpu.SMEM)
VMEM = pl.BlockSpec(memory_space=pltpu.VMEM)
ANY = pl.BlockSpec(memory_space=pl.ANY)
GRP, QUARTER, SOURCE, ORBITAL = 0, 1, 2, 3


def params():
    return pltpu.CompilerParams(vmem_limit_bytes=VMEM_CAP)


def cost(flops, moved):
    return pl.CostEstimate(flops=flops, bytes_accessed=moved, transcendentals=0)


def swapped(value, axis, mask):
    pairs = [(source, source ^ mask) for source in range(lax.axis_size(axis))]
    return lax.ppermute(value, axis, pairs)


def forwarded(value):
    total = lax.axis_size(BOTH)
    pairs = [(p, (p + 2) % total if p % 2 == 0 else (p - 2) % total) for p in range(total)]
    return lax.ppermute(value, BOTH, pairs)


def table_of_integers():
    n_grp, n_blk = lax.axis_size("grp"), lax.axis_size("blk")
    total = n_grp * n_blk
    g, b = lax.axis_index("grp"), lax.axis_index("blk")
    place = g * n_blk + b
    source = jnp.where(place % 2 == 0, (place - 2) % total, (place + 2) % total) // n_blk
    slot = jnp.arange(8, dtype=jnp.int32)
    spot = slot - ORBITAL
    partner = jnp.where((place - spot) % 2 == 0, (place - spot) % total, (place + spot) % total)
    orbital = partner % n_blk * n_grp + partner // n_blk
    table = jnp.where(slot == GRP, g, jnp.where(slot == QUARTER, b % 4, jnp.where(slot == SOURCE, source, orbital)))
    return table.astype(jnp.int32)


def pack_kernel(n_grp, table_ref, metric_ref, out_ref, sems):
    chunk = metric_ref.shape[0] // n_grp // 4
    copies = []
    for j in range(n_grp // 2 + 1):
        row = (((table_ref[GRP] + j) % n_grp) * 4 + table_ref[QUARTER]) * chunk
        copies.append(
            pltpu.make_async_copy(
                metric_ref.at[pl.ds(pl.multiple_of(row, chunk), chunk), :],
                out_ref.at[pl.ds(j * chunk, chunk), :],
                sems.at[j],
            )
        )
        copies[-1].start()
    for copy in copies:
        copy.wait()


def pack(metric, table, n_grp):
    rows, cols = metric.shape
    count = n_grp // 2 + 1
    return pl.pallas_call(
        functools.partial(pack_kernel, n_grp),
        in_specs=[SMEM, ANY],
        out_specs=VMEM,
        out_shape=jax.ShapeDtypeStruct((count * (rows // n_grp // 4), cols), metric.dtype),
        scratch_shapes=[pltpu.SemaphoreType.DMA((count,))],
        name="pack",
    )(table, metric)


def unpack_kernel(n_grp, table_ref, *refs):
    parts, out_ref = refs[:-1], refs[-1]
    width = out_ref.shape[0] // n_grp
    chunk = width // 4
    g, q = table_ref[GRP], table_ref[QUARTER]

    def place(m, carry):
        for at, part in enumerate(parts):
            odd, dq = at % 2, at // 2
            s = g ^ (2 * m + odd)
            cols = pl.ds(pl.multiple_of(s * width, width), width)
            for j in range(n_grp // 2 + 1):
                a = (s + j) % n_grp
                rows = pl.ds(pl.multiple_of(a * width + (q ^ dq) * chunk, chunk), chunk)
                out_ref[rows, cols] = part[m, j * chunk : (j + 1) * chunk, :]
        return carry

    lax.fori_loop(0, n_grp // 2, place, 0)

    def mirror(s, carry):
        here = pl.ds(pl.multiple_of(s * width, width), width)
        for j in range(1, n_grp // 2):
            there = pl.ds(pl.multiple_of(((s + j) % n_grp) * width, width), width)
            out_ref[here, there] = out_ref[there, here].T
        return carry

    lax.fori_loop(0, n_grp, mirror, 0)


def unpack(parts, table, n_grp):
    width = parts[0].shape[2]
    size = n_grp * width
    return pl.pallas_call(
        functools.partial(unpack_kernel, n_grp),
        in_specs=[SMEM] + [VMEM] * len(parts),
        out_specs=VMEM,
        out_shape=jax.ShapeDtypeStruct((size, size), parts[0].dtype),
        compiler_params=params(),
        cost_estimate=cost(0, 4 * size * size),
        name="unpack",
    )(table, *parts)


def fit_kernel(which, first, has_base, table_ref, metric_ref, *refs):
    refs = list(refs)
    base_ref = refs.pop(0) if has_base else None
    raw_ref = refs.pop()
    out_ref = refs.pop()
    per, width, _ = refs[0].shape
    run = per * width
    high, low = table_ref[which] // per, table_ref[which] % per
    every = len(refs) * run == metric_ref.shape[1]
    blocks = [high ^ (i + first) for i in range(len(refs))]
    for i, group in enumerate(refs):
        for j in range(per):
            row = pl.multiple_of(blocks[i] * run, run) + j * width if every else i * run + j * width
            raw_ref[pl.ds(row, width), :] = group[j ^ low]
    for r in range(0, out_ref.shape[0], TILE):
        rows = slice(r, r + TILE)
        if every:
            total = jnp.dot(metric_ref[rows, :], raw_ref[...], preferred_element_type=F32)
        else:
            total = None
            for i, block in enumerate(blocks):
                cols = pl.ds(pl.multiple_of(block * run, run), run)
                part = jnp.dot(metric_ref[rows, cols], raw_ref[i * run : (i + 1) * run, :], preferred_element_type=F32)
                total = part if total is None else total + part
        if has_base:
            total = total + base_ref[rows, :]
        out_ref[rows, :] = total.astype(out_ref.dtype)


def fit(metric, groups, table, which, first=0, base=None, partial=False):
    size = metric.shape[0]
    per, width, nv = groups[0].shape
    depth = per * width * len(groups)
    given = [metric] + ([base] if base is not None else []) + list(groups)
    return pl.pallas_call(
        functools.partial(fit_kernel, which, first, base is not None),
        in_specs=[SMEM] + [VMEM] * len(given),
        out_specs=VMEM,
        out_shape=jax.ShapeDtypeStruct((size, nv), F32 if partial else BF16),
        scratch_shapes=[pltpu.VMEM((depth, nv), BF16)],
        compiler_params=params(),
        cost_estimate=cost(2 * size * depth * nv, 2 * size * depth),
        name="fit",
    )(table, *given)


def tilde_into(tilde_ref, amp_ref, coulomb_ref, esum, virt_ref):
    nv = amp_ref.shape[0]
    slab = 128
    cuts = range(0, nv, slab)
    for r in cuts:
        mine = jnp.broadcast_to(virt_ref[:, r : r + slab], (slab, slab)).T
        for c in cuts:
            denom = esum - mine - virt_ref[:, c : c + slab]
            amp_ref[r : r + slab, c : c + slab] = coulomb_ref[r : r + slab, c : c + slab] / denom
    energy = jnp.float32(0)
    for r in cuts:
        tilde = 2.0 * amp_ref[r : r + slab, :] - amp_ref[:, r : r + slab].T
        energy += jnp.sum(coulomb_ref[r : r + slab, :] * tilde)
        tilde_ref[r : r + slab, :] = tilde.astype(BF16)
    return energy


def pair_kernel(visits, has_base, final, known, *refs):
    refs = list(refs)
    take = lambda count: [refs.pop(0) for _ in range(count)]
    table_ref, occ_ref, virt_ref, own_ref = take(4)
    others = take(len(visits))
    base_ref = take(1)[0] if has_base else None
    known_refs = take(len(known))
    energy_ref, dens_ref, coulomb_ref, amp_ref = take(4)
    tildes = take(len(visits))
    e_own = occ_ref[table_ref[ORBITAL]]
    for ref, (start, count) in zip(known_refs, known):
        for i in range(count):
            energy_ref[0, start + i] = ref[0, i]
    for at, visit in enumerate(visits):
        coulomb_ref[...] = lax.dot_general(
            own_ref[...], others[at][...], (((0,), (0,)), ((), ())), preferred_element_type=F32
        )
        esum = e_own + occ_ref[table_ref[ORBITAL + visit]]
        energy = tilde_into(tildes[at], amp_ref, coulomb_ref, esum, virt_ref)
        energy_ref[0, visit if final else at] = energy
    if final:
        stage_ref, sems = refs
        ways = own_ref.shape[1] // dens_ref.shape[1]
        copies = []
    for r in range(0, own_ref.shape[0], TILE):
        rows = slice(r, r + TILE)
        total = base_ref[rows, :] if has_base else None
        for other, tilde in zip(others, tildes):
            part = lax.dot_general(
                other[rows, :], tilde[...], (((1,), (1,)), ((), ())), preferred_element_type=F32
            )
            total = part if total is None else total + part
        if final:
            lanes = dens_ref.shape[1]
            for c in range(ways):
                stage_ref[pl.ds(r * ways + c, TILE, stride=ways), :] = total[:, c * lanes : (c + 1) * lanes]
            cut = pl.ds(r * ways, TILE * ways)
            copies.append(pltpu.make_async_copy(stage_ref.at[cut, :], dens_ref.at[cut, :], sems.at[r // TILE]))
            copies[-1].start()
        else:
            dens_ref[rows, :] = total
    if final:
        for copy in copies:
            copy.wait()


def pairs(own, others, visits, table, occ, virt, base=None, final=False, known=()):
    size, nv = own.shape
    lanes = 128
    given = [own, *others] + ([base] if base is not None else [])
    shape = (size * nv // lanes, lanes) if final else (size, nv)
    scratch = [pltpu.VMEM((nv, nv), F32)] * 2 + [pltpu.VMEM((nv, nv), BF16)] * len(visits)
    if final:
        scratch += [pltpu.VMEM(shape, F32), pltpu.SemaphoreType.DMA((size // TILE,))]
    return pl.pallas_call(
        functools.partial(
            pair_kernel, tuple(visits), base is not None, final, tuple((start, count) for start, count, _ in known)
        ),
        in_specs=[SMEM, SMEM, VMEM] + [VMEM] * len(given) + [SMEM] * len(known),
        out_specs=[SMEM, ANY if final else VMEM],
        out_shape=[
            jax.ShapeDtypeStruct((1, VISITS if final else len(visits)), F32),
            jax.ShapeDtypeStruct(shape, F32),
        ],
        scratch_shapes=scratch,
        compiler_params=params(),
        cost_estimate=cost(4 * size * nv * nv * len(visits), 4 * size * nv),
        name="pairs",
    )(table, occ, virt, *given, *(energy for _, _, energy in known))


def body(raw_ints, metric, occ_energy, virt_energy):
    n_grp = lax.axis_size("grp")
    per = n_grp // GROUPS
    g = lax.axis_index("grp")
    table = table_of_integers()

    mine = pack(metric, table, n_grp)
    even = jnp.stack([mine] + [swapped(mine, "grp", k) for k in range(2, n_grp, 2)])
    odd = swapped(even, "grp", 1)
    even_y = swapped(even, "blk", 2)
    odd_y = swapped(odd, "blk", 2)
    parts = [even, odd, swapped(even, "blk", 1), swapped(odd, "blk", 1), even_y, odd_y]
    parts += [swapped(even_y, "blk", 1), swapped(odd_y, "blk", 1)]
    full = unpack(parts, table, n_grp)

    by_orbital = lax.optimization_barrier(jnp.transpose(raw_ints, (1, 0, 2)))
    got = [lax.dynamic_index_in_dim(by_orbital, g ^ k, 0, keepdims=False) for k in range(n_grp)]
    got = got[:1] + [swapped(got[k], "grp", k) for k in range(1, n_grp)]
    groups = [jnp.stack(got[i * per : (i + 1) * per]) for i in range(GROUPS)]
    next_groups = [forwarded(group) for group in groups]

    own = fit(full, groups, table, GRP)
    mate = swapped(own, "blk", 1)
    some = fit(full, next_groups[:-1], table, SOURCE, partial=True)
    next_ = fit(full, next_groups[-1:], table, SOURCE, first=GROUPS - 1, base=some)
    next_mate = swapped(next_, "blk", 1)

    virt = virt_energy[None, :]
    energy_a, base = pairs(own, [own, mate], [0, 1], table, occ_energy, virt)
    energy_b, base = pairs(own, [next_], [2], table, occ_energy, virt, base=base)
    energy, density = pairs(
        own,
        [next_mate],
        [3],
        table,
        occ_energy,
        virt,
        base=base,
        final=True,
        known=[(0, 2, energy_a), (2, 1, energy_b)],
    )
    size, nv = own.shape
    return density.reshape(size, 1, nv), energy


def solution(mesh):
    in_specs = (P("grp", "blk", None), P(None, "grp"), P(), P())
    out_specs = (P(None, ("blk", "grp"), None), P(("blk", "grp"), None))
    return jax.shard_map(body, mesh=mesh, in_specs=in_specs, out_specs=out_specs, check_vma=False)
```
